32 devices in a mesh: ctx: 16 (over z, y, core), sec: 2 (over x).
Axes of the slice: x: 2, y: 2, z: 4, core: 2. Of those that a mesh axis runs over, the one named last changes fastest.
Arguments:
- queries: bfloat16 [1024, 6144], P('ctx', 'sec'), may hold values from -128 to 128
- keys: bfloat16 [1280, 1024], P('ctx', 'sec'), may hold values from -8 to 8
- values: bfloat16 [1280, 1024], P('ctx', 'sec'), may hold values from -6 to 6
- gain: float32 [6144], P('sec'), may hold values from 0.5 to 1.5
- router: float32 [6144, 8], P('sec'), may hold values from -0.078125 to 0.078125
- w_gate: bfloat16 [6144, 16384], P('sec', 'ctx'), may hold values from -0.078125 to 0.078125
- w_up: bfloat16 [6144, 16384], P('sec', 'ctx'), may hold values from -0.078125 to 0.078125
- w_down: bfloat16 [16384, 6144], P('ctx', 'sec'), may hold values from -0.125 to 0.125
- routes: int32 [1024, 2], P('ctx'), may hold values from 0 to 7, all different within a row; in each aligned block of 64 rows (0 to 63, 64 to 127, ...) at most 20 rows name the same one
Outputs:
- normed: bfloat16 [1024, 6144], P('ctx', 'sec')
- moe_out: bfloat16 [1024, 6144], P('ctx', 'sec')
The draws below stay inside these ranges and needn't reach their ends.
Inputs may be any that keep to these rules, and one draw needn't show every extreme that they name: `routes`: each row names 2 different experts. Among the rows at one index of ctx no expert is named more than 20 times, and in every draw some expert is named exactly 20 times there.
All inputs are finite; a program needn't handle non-finite values.
Results may differ from the reference program's by a relative error of at most 0.023.
Values may be sent and summed in bfloat16 or wider, within the bound.
A program may use at most 192 MiB of HBM per device.

```python
import math
import jax
import jax.numpy as jnp
import numpy as np
from jax import lax

D = 6144
HEADS = 48
KV_HEADS = 8
HEAD_DIM = 128
EXPERTS = 8
TOP = 2
FF_DEV = 1024
TOK = 64
CAP = 20
GROUP = 2
FF = 2048
TOKENS = 1024
LEN = 1280
N_CTX = 16


def key_base(key):
    fresh = jax.random.normal(jax.random.fold_in(key, 71), (LEN, KV_HEADS * HEAD_DIM), jnp.float32)
    return jnp.clip(fresh, -6.0, 6.0)


def draw_keys(key, part):
    base = key_base(key)
    return base.astype(jnp.bfloat16)


def draw_queries(key, part):
    fresh = jax.random.normal(jax.random.fold_in(key, 72), (TOKENS, HEADS * HEAD_DIM), jnp.float32)
    fresh = jnp.clip(fresh, -6.0, 6.0)
    return fresh.astype(jnp.bfloat16)


def steps_of(key, extent, pieces, low, high):
    level, own = 1.0, jax.random.fold_in(key, 6)
    for axis_at, shards_of in pieces:
        heights = jnp.exp(jax.random.uniform(jax.random.fold_in(own, axis_at), (shards_of,), jnp.float32, low / len(pieces), high / len(pieces)))
        level = level * jnp.repeat(heights, extent[axis_at] // shards_of).reshape([-1 if axis == axis_at else 1 for axis in range(len(extent))])
    return level


def deal_out(key, own, number, rows, number_of, top, most, lean):
    order = jax.random.permutation(key, number_of)
    heavy_load, common = shares(number_of, rows * top, most, lean, True), shares(number_of, rows * top, most, lean, False)
    places = jnp.arange(number_of)

    def named(lengths, offset_by):
        used = int((lengths > 0).sum())
        fixed = max(1, used // 4)
        shifted = fixed + (places - fixed + offset_by * (used - fixed)) % max(1, number_of - fixed)
        return jnp.zeros((number_of,), jnp.int32).at[order[jnp.where(places < fixed, places, shifted)]].set(jnp.asarray(lengths, jnp.int32))

    lengths = jnp.where(number % 4 == 0, named(heavy_load, number // 4), named(common, number - number // 4 - 1))
    mixed = jax.random.permutation(jax.random.fold_in(own, 3), number_of)
    giver, sink = mixed[0:number_of // 2 * 2:2], mixed[1:number_of // 2 * 2:2]
    margin = jnp.minimum(lengths[giver] - 1, most - lengths[sink]) // 2
    margin = jnp.where((giver == order[0]) | (sink == order[0]) | (lengths[sink] == 0), 0, jnp.maximum(margin, 0))
    shifted = jax.random.randint(jax.random.fold_in(own, 4), (number_of // 2,), 0, 1 << 20) % (margin + 1)
    lengths = lengths.at[giver].add(-shifted).at[sink].add(shifted)
    labels = jnp.searchsorted(jnp.cumsum(lengths), jnp.arange(rows * top), side="right").astype(jnp.int32)
    grid = labels.reshape(top, rows).T
    grid = grid[jax.random.permutation(jax.random.fold_in(own, 1), rows)]
    offset_by = jax.random.randint(jax.random.fold_in(own, 2), (rows, 1), 0, top)
    return jnp.take_along_axis(grid, (jnp.arange(top)[None, :] + offset_by) % top, axis=1)


def shares(count, total, bound, slope, full):
    loads = [(1 << 20) // math.isqrt(rank ** slope) + 1 for rank in range(1, count + 1)]
    largest = bound if full else min(bound, max(-(-total // count), total * loads[0] // sum(loads)))
    least = 1 if total - largest >= count - 1 else 0
    given, spare = [largest] + [least] * (count - 1), total - largest - least * (count - 1)
    while spare > 0:
        candidates = [i for i in range(1, count) if given[i] < largest] or [i for i in range(1, count) if given[i] < bound]
        whole, left = sum([loads[i] for i in candidates]), spare
        for i in candidates:
            extra = min(bound - given[i], max(1, left * loads[i] // whole), spare)
            given[i] = given[i] + extra
            spare = spare - extra
    return np.array(given)


def noise(stream_key, dims, scale, bound, pieces=(), kind=jnp.bfloat16):
    drawn = scale * jax.random.normal(stream_key, dims, jnp.float32)
    if pieces:
        drawn = drawn * steps_of(stream_key, dims, pieces, -0.22, 0.18)
    return jnp.clip(drawn, -bound, bound).astype(kind)


def setup_inputs(seed: int = 0) -> dict:
    splits = jax.random.split(jax.random.key(seed), 10)
    queries = draw_queries(jax.random.fold_in(splits[9], 71), 0)
    keys = draw_keys(jax.random.fold_in(splits[9], 71), 0)
    values = noise(splits[2], (LEN, KV_HEADS * HEAD_DIM), 1.0, 6.0, ((0, 16), (1, 2)))
    gain = jnp.clip(1.0 + 0.1 * jax.random.normal(splits[3], (D,), jnp.float32), 0.5, 1.5)
    router = noise(splits[4], (D, EXPERTS), D ** -0.5, 0.078125, ((0, 2),), jnp.float32)
    w_gate = noise(splits[5], (D, EXPERTS * FF), D ** -0.5, 0.078125, ((0, 2), (1, 16)))
    w_up = noise(splits[6], (D, EXPERTS * FF), D ** -0.5, 0.078125, ((0, 2), (1, 16)))
    w_down = noise(splits[7], (EXPERTS * FF, D), FF ** -0.5, 0.125, ((0, 16), (1, 2)))
    routes_keys = jax.random.split(jax.random.fold_in(splits[8], 1), TOKENS // TOK)
    routes_turns = jax.random.permutation(jax.random.fold_in(splits[8], 3), TOKENS // TOK)
    routes = jax.vmap(lambda own, number: deal_out(jax.random.fold_in(splits[8], 2), own, number, TOK, EXPERTS, TOP, CAP, 1))(routes_keys, routes_turns).reshape((TOKENS, TOP))
    return {"queries": queries, "keys": keys, "values": values, "gain": gain, "router": router, "w_gate": w_gate, "w_up": w_up, "w_down": w_down, "routes": routes}


def expert_slots(routes):
    flat = routes.reshape(N_CTX, TOK * TOP)
    hot = (flat[:, :, None] == jnp.arange(EXPERTS, dtype=jnp.int32)[None, None, :]).astype(jnp.int32)
    before = jnp.cumsum(hot, axis=1) - hot
    return lax.optimization_barrier(jnp.sum(before * hot, axis=2)).astype(jnp.int32)

def reference(queries, keys, values, gain, router, w_gate, w_up, w_down, routes):
    cache = LEN - TOKENS
    query_pos = cache + jnp.arange(TOKENS, dtype=jnp.int32)
    visible = jnp.arange(LEN, dtype=jnp.int32)[None, :] <= query_pos[:, None]
    scale_factor = 1.0 / math.sqrt(HEAD_DIM)
    group_size = HEADS // KV_HEADS

    def one_head(head):
        kv_head = head // group_size
        query_head = lax.dynamic_slice_in_dim(queries, head * HEAD_DIM, HEAD_DIM, 1)
        key_head = lax.dynamic_slice_in_dim(keys, kv_head * HEAD_DIM, HEAD_DIM, 1)
        value_head = lax.dynamic_slice_in_dim(values, kv_head * HEAD_DIM, HEAD_DIM, 1)
        scores = jnp.dot(query_head, key_head.T, preferred_element_type=jnp.float32) * scale_factor
        scores = jnp.where(visible, scores, -1e+30)
        largest = lax.optimization_barrier(jnp.max(scores, axis=1, keepdims=True))
        weights = jnp.where(visible, jnp.exp(scores - largest), 0.0)
        total = lax.optimization_barrier(jnp.sum(weights, axis=1, keepdims=True))
        mixed = jnp.dot(weights.astype(jnp.bfloat16), value_head, preferred_element_type=jnp.float32)
        return (mixed / total).astype(jnp.bfloat16)
    heads_out = lax.map(one_head, jnp.arange(HEADS, dtype=jnp.int32))
    attended = jnp.transpose(heads_out, (1, 0, 2)).reshape(TOKENS, D)
    attn_float = attended.astype(jnp.float32)
    gained = attn_float * gain[None, :]
    squares = lax.optimization_barrier(jnp.sum(attn_float * attn_float, axis=1))
    factor = lax.rsqrt(squares / D + 1e-05)
    normed = (gained * factor[:, None]).astype(jnp.bfloat16)
    logits = factor[:, None] * jnp.dot(gained, router, precision=lax.Precision.HIGHEST)
    chosen = jnp.take_along_axis(logits, routes, axis=1)
    combine = 1.0 / lax.optimization_barrier(jnp.sum(jnp.exp(chosen[:, None, :] - chosen[:, :, None]), axis=2))
    slots = expert_slots(routes).reshape(TOKENS, TOP)
    source = jnp.broadcast_to((jnp.arange(TOKENS, dtype=jnp.int32) // TOK)[:, None], (TOKENS, TOP))
    filled = jnp.broadcast_to(normed[:, None, :], (TOKENS, TOP, D))
    buffer = jnp.zeros((EXPERTS, N_CTX, CAP, D), jnp.bfloat16).at[routes, source, slots].set(filled)

    def one_expert(expert):
        rows = buffer[expert].reshape(N_CTX * CAP, D)
        gate = jnp.dot(rows, lax.dynamic_slice_in_dim(w_gate, expert * FF, FF, 1), preferred_element_type=jnp.float32)
        upward = jnp.dot(rows, lax.dynamic_slice_in_dim(w_up, expert * FF, FF, 1), preferred_element_type=jnp.float32)
        hidden = (jax.nn.silu(gate) * upward).astype(jnp.bfloat16)
        down_rows = lax.dynamic_slice_in_dim(w_down, expert * FF, FF, 0)
        parts = jnp.einsum('rgf,gfd->grd', hidden.reshape(N_CTX * CAP, GROUP, FF_DEV).astype(jnp.float32), down_rows.reshape(GROUP, FF_DEV, D).astype(jnp.float32), precision=lax.Precision.HIGHEST)
        parts = lax.optimization_barrier(parts.astype(jnp.bfloat16)).astype(jnp.float32)
        return lax.optimization_barrier(jnp.sum(parts, axis=0)).reshape(N_CTX, CAP, D)
    expert_out = lax.map(one_expert, jnp.arange(EXPERTS, dtype=jnp.int32))
    picked = expert_out[routes, source, slots]
    moe_out = lax.optimization_barrier(jnp.sum(picked * combine[:, :, None], axis=1)).astype(jnp.bfloat16)
    return (normed, moe_out)
```

```python
import functools
import math

import jax
import jax.numpy as jnp
import numpy as np
from jax import lax
from jax.experimental import pallas as pl
from jax.experimental.pallas import tpu as pltpu
from jax.sharding import PartitionSpec as P

D = 6144
HEADS = 48
KV_HEADS = 8
HEAD_DIM = 128
EXPERTS = 8
TOP = 2
CAP = 20
SPLIT = 4
UNIT = CAP * SPLIT
CHUNKS = 2
PAIR = 4
MESH = pl.DeviceIdType.MESH


def on_ctx(index):
    return {"ctx": index}


def attend_kernel(n, q_hbm, k_hbm, v_hbm, out_ref, q_ref, kv, local_sem, z_send, y_send, c_send, recv):
    me = lax.axis_index("ctx")
    far = n // 4
    zi, yi, ci = me // 4, (me // 2) % 2, me % 2
    rows = k_hbm.shape[0]

    def slot(source):
        return kv.at[:, pl.ds(pl.multiple_of(source * rows, 16), rows), :]

    mine = pl.ds(pl.multiple_of(me * rows, 16), rows)
    loads = [
        pltpu.make_async_copy(k_hbm, kv.at[0, mine, :], local_sem.at[0]),
        pltpu.make_async_copy(v_hbm, kv.at[1, mine, :], local_sem.at[1]),
        pltpu.make_async_copy(q_hbm, q_ref, local_sem.at[2]),
    ]
    for load in loads:
        load.start()
    y_peer = zi * 4 + (1 - yi) * 2 + ci
    c_peer = zi * 4 + yi * 2 + 1 - ci
    barrier = pltpu.get_barrier_semaphore()
    for k in range(1, far):
        pl.semaphore_signal(
            barrier, inc=1, device_id=on_ctx(((zi + k) % far) * 4 + yi * 2 + ci), device_id_type=MESH
        )
    for peer in (y_peer, c_peer):
        pl.semaphore_signal(barrier, inc=1, device_id=on_ctx(peer), device_id_type=MESH)
    pl.semaphore_wait(barrier, far + 1)
    loads[0].wait()
    loads[1].wait()
    sent = []

    def send(source, peer, sem):
        copy = pltpu.make_async_remote_copy(
            src_ref=slot(source), dst_ref=slot(source), send_sem=sem, recv_sem=recv.at[source],
            device_id=on_ctx(peer), device_id_type=MESH,
        )
        copy.start()
        sent.append(copy)

    def arrived(source):
        pltpu.make_async_remote_copy(
            src_ref=slot(source), dst_ref=slot(source), send_sem=c_send.at[0], recv_sem=recv.at[source],
            device_id=on_ctx(c_peer), device_id_type=MESH,
        ).wait_recv()

    for k in range(1, far):
        send(me, ((zi + k) % far) * 4 + yi * 2 + ci, z_send.at[k - 1])
    send(me, y_peer, y_send.at[0])
    send(me, c_peer, c_send.at[0])
    for k in range(1, far):
        source = ((zi + far - k) % far) * 4 + yi * 2 + ci
        arrived(source)
        send(source, y_peer, y_send.at[k])
        send(source, c_peer, c_send.at[k])
    for k in range(far):
        source = ((zi + far - k) % far) * 4 + (1 - yi) * 2 + ci
        arrived(source)
        send(source, c_peer, c_send.at[far + k])
    for k in range(far):
        for y in range(2):
            arrived(((zi + far - k) % far) * 4 + y * 2 + 1 - ci)
    loads[2].wait()

    tokens = q_ref.shape[0]
    group = HEADS // KV_HEADS
    length = n * rows
    position = (rows - tokens) * n + me * tokens + lax.broadcasted_iota(jnp.int32, (tokens, length), 0)
    visible = lax.broadcasted_iota(jnp.int32, (tokens, length), 1) <= position
    scale_factor = 1.0 / math.sqrt(HEAD_DIM)

    def one_head(g, carry):
        at = pl.ds(pl.multiple_of(g * HEAD_DIM, HEAD_DIM), HEAD_DIM)
        k, v = kv[0, :, at], kv[1, :, at]
        for h in range(group):
            cols = pl.ds(pl.multiple_of(g * group * HEAD_DIM + h * HEAD_DIM, HEAD_DIM), HEAD_DIM)
            s = lax.dot_general(
                q_ref[:, cols], k, (((1,), (1,)), ((), ())), preferred_element_type=jnp.float32
            )
            s = jnp.where(visible, s * scale_factor, -1e30)
            w = jnp.where(visible, jnp.exp(s - jnp.max(s, axis=1, keepdims=True)), 0.0)
            total = jnp.sum(w, axis=1, keepdims=True)
            mixed = jnp.dot(w.astype(jnp.bfloat16), v, preferred_element_type=jnp.float32)
            out_ref[:, cols] = (mixed / total).astype(jnp.bfloat16)
        return carry

    lax.fori_loop(0, k_hbm.shape[1] // HEAD_DIM, one_head, 0)
    for copy in sent:
        copy.wait_send()


def attend(queries, keys, values, n):
    rows, width = keys.shape
    any_spec = pl.BlockSpec(memory_space=pl.ANY)
    return pl.pallas_call(
        functools.partial(attend_kernel, n),
        out_shape=jax.ShapeDtypeStruct(queries.shape, jnp.bfloat16),
        in_specs=[any_spec] * 3,
        out_specs=pl.BlockSpec(memory_space=pltpu.VMEM),
        scratch_shapes=[
            pltpu.VMEM(queries.shape, jnp.bfloat16),
            pltpu.VMEM((2, n * rows, width), jnp.bfloat16),
            pltpu.SemaphoreType.DMA((3,)),
            pltpu.SemaphoreType.DMA((n // 4,)),
            pltpu.SemaphoreType.DMA((n // 4,)),
            pltpu.SemaphoreType.DMA((n // 2,)),
            pltpu.SemaphoreType.DMA((n,)),
        ],
        compiler_params=pltpu.CompilerParams(
            collective_id=0, has_side_effects=True, vmem_limit_bytes=48 << 20
        ),
        name="attend",
    )(queries, keys, values)


def experts_kernel(
    n, normed, place, mix, order, order_t, w_gate, w_up, w_down, out_ref,
    gate_w, up_w, down_w, packed, disp, rows_x, gu_send, gu_own, gu_recv, hidden, parts, group_parts,
    back, returned, w_sem, own_sem, d_send, f_send, d_recv, x_send, x_recv, h_send, h_recv,
    g_send, g_recv, r_send, r_recv,
):
    me, sec = lax.axis_index("ctx"), lax.axis_index("sec")
    members = n // EXPERTS
    block = EXPERTS // CHUNKS
    e, j = me // members, me % members
    b, el = e // block, e % block
    width = packed.shape[2]
    half = gate_w.shape[1] // 2
    chunk_rows = block * members * CAP
    tile = 256

    loads = [
        pltpu.make_async_copy(w_gate, gate_w, w_sem.at[0]),
        pltpu.make_async_copy(w_up, up_w, w_sem.at[1]),
        pltpu.make_async_copy(w_down, down_w, w_sem.at[2]),
    ]
    for load in loads:
        load.start()

    def expert_at(q, i, sign):
        return ((b + CHUNKS + sign * q) % CHUNKS) * block + (el + block + sign * i) % block

    others = [(q, i) for q in range(CHUNKS) for i in range(block) if (q, i) != (0, 0)]
    barrier = pltpu.get_barrier_semaphore()
    for q, i in others:
        pl.semaphore_signal(
            barrier, inc=1, device_id=on_ctx(expert_at(q, i, 1) * members + j), device_id_type=MESH
        )
    for g in range(1, members):
        pl.semaphore_signal(
            barrier, inc=1, device_id=on_ctx(e * members + (j + g) % members), device_id_type=MESH
        )
    pl.semaphore_signal(barrier, inc=1, device_id={"sec": 1 - sec}, device_id_type=MESH)

    stacked = jnp.concatenate([normed[:, c * width:(c + 1) * width] for c in range(SPLIT)], axis=0)
    for x in range(EXPERTS):
        packed[x] = jnp.dot(
            place[x * UNIT:(x + 1) * UNIT, :], stacked, preferred_element_type=jnp.float32
        ).astype(jnp.bfloat16)
    pl.semaphore_wait(barrier, EXPERTS - 1 + members)

    sent = []

    def remote(src, dst, send_sem, recv_sem, device):
        return pltpu.make_async_remote_copy(
            src_ref=src, dst_ref=dst, send_sem=send_sem, recv_sem=recv_sem,
            device_id=device, device_id_type=MESH,
        )

    def send(src, dst, send_sem, recv_sem, device):
        copy = remote(src, dst, send_sem, recv_sem, device)
        copy.start()
        sent.append(copy)

    def wait_for(dst, recv_sem):
        remote(dst, dst, d_send.at[0], recv_sem, {"sec": 1 - sec}).wait_recv()

    for number, (q, i) in enumerate(others):
        target = expert_at(q, i, 1)
        send(packed.at[target], disp.at[me], d_send.at[number], d_recv.at[me], on_ctx(target * members + j))
    own = pltpu.make_async_copy(packed.at[e], disp.at[me], own_sem.at[0])
    own.start()
    for g in range(1, members):
        send(
            packed.at[e], disp.at[me], f_send.at[0, g - 1], d_recv.at[me],
            on_ctx(e * members + (j + g) % members),
        )

    def first_slot(q):
        return ((b + CHUNKS - q) % CHUNKS) * block * members

    def forward(q):
        for i in range(block):
            if (q, i) == (0, 0):
                continue
            source = expert_at(q, i, -1) * members + j
            wait_for(disp.at[source], d_recv.at[source])
            for g in range(1, members):
                send(
                    disp.at[source], disp.at[source], f_send.at[q * block + i, g - 1], d_recv.at[source],
                    on_ctx(e * members + (j + g) % members),
                )

    def gate_up(q):
        if q == 0:
            own.wait()
        for i in range(block):
            for g in range(1, members):
                source = expert_at(q, i, -1) * members + (j + g) % members
                wait_for(disp.at[source], d_recv.at[source])
        first = first_slot(q)
        for u in range(block * members // PAIR):
            flat = disp[pl.ds(first + u * PAIR, PAIR)].reshape(PAIR * UNIT, width)
            tall = jnp.dot(order[...], flat, preferred_element_type=jnp.float32).astype(jnp.bfloat16)
            for c in range(SPLIT):
                rows_x[u * PAIR * CAP:(u + 1) * PAIR * CAP, c * width:(c + 1) * width] = tall[
                    c * PAIR * CAP:(c + 1) * PAIR * CAP
                ]
        if q == 0:
            loads[0].wait()
            loads[1].wait()

        def product(weights, base, t):
            at = pl.ds(pl.multiple_of(base + t * tile, tile), tile)
            return jnp.dot(rows_x[...], weights[:, at], preferred_element_type=jnp.float32)

        def peers(t, carry):
            at = pl.multiple_of(t * tile, tile)
            gu_send[q, :, pl.ds(at, tile)] = product(gate_w, (1 - sec) * half, t).astype(jnp.bfloat16)
            gu_send[q, :, pl.ds(at + half, tile)] = product(up_w, (1 - sec) * half, t).astype(jnp.bfloat16)
            return carry

        def mine(t, carry):
            at = pl.multiple_of(t * tile, tile)
            gu_own[q, :, pl.ds(at, tile)] = product(gate_w, sec * half, t)
            gu_own[q, :, pl.ds(at + half, tile)] = product(up_w, sec * half, t)
            return carry

        lax.fori_loop(0, half // tile, peers, 0)
        send(gu_send.at[q], gu_recv.at[q], x_send.at[q], x_recv.at[q], {"sec": 1 - sec})
        lax.fori_loop(0, half // tile, mine, 0)

    def activate(q):
        wait_for(gu_recv.at[q], x_recv.at[q])
        full = gu_own[q] + gu_recv[q].astype(jnp.float32)
        gate, up = full[:, :half], full[:, half:]
        hidden[sec, q] = (gate / (1.0 + jnp.exp(-gate)) * up).astype(jnp.bfloat16)
        send(hidden.at[sec, q], hidden.at[sec, q], h_send.at[q], h_recv.at[q], {"sec": 1 - sec})

    def down(q):
        wait_for(hidden.at[1 - sec, q], h_recv.at[q])
        if q == 0:
            loads[2].wait()
        first = first_slot(q)
        both = jnp.concatenate([hidden[0, q], hidden[1, q]], axis=1)
        wide = [
            jnp.dot(both, down_w[:, c * width:(c + 1) * width], preferred_element_type=jnp.float32).astype(
                jnp.bfloat16
            )
            for c in range(SPLIT)
        ]
        for u in range(block * members // PAIR):
            tall = jnp.concatenate([w[u * PAIR * CAP:(u + 1) * PAIR * CAP] for w in wide], axis=0)
            flat = jnp.dot(order_t[...], tall, preferred_element_type=jnp.float32).astype(jnp.bfloat16)
            for s in range(PAIR):
                at = first + u * PAIR + s
                parts[at // members, at % members] = flat[s * UNIT:(s + 1) * UNIT]
        start = first // members
        for g in range(1, members):
            to = (j + g) % members
            send(
                parts.at[pl.ds(start, block), to], group_parts.at[g - 1, pl.ds(start, block)],
                g_send.at[q, g - 1], g_recv.at[q, g - 1], on_ctx(e * members + to),
            )

    def give_back(q):
        start = first_slot(q) // members
        for g in range(1, members):
            wait_for(group_parts.at[g - 1, pl.ds(start, block)], g_recv.at[q, g - 1])
        for i in range(block):
            source = expert_at(q, i, -1)
            total = parts[source, j].astype(jnp.float32)
            for g in range(1, members):
                total = total + group_parts[g - 1, source].astype(jnp.float32)
            if (q, i) == (0, 0):
                returned[e] = total.astype(jnp.bfloat16)
            else:
                back[source] = total.astype(jnp.bfloat16)
                send(
                    back.at[source], returned.at[e], r_send.at[q * block + i], r_recv.at[e],
                    on_ctx(source * members + j),
                )

    stages = (forward, gate_up, activate, down, give_back)
    lag = (0, 0, 1, 1, 2)
    for step in range(CHUNKS + max(lag)):
        for stage, delay in sorted(zip(stages, lag), key=lambda pair: pair[1]):
            if 0 <= step - delay < CHUNKS:
                stage(step - delay)

    for q, i in others:
        target = expert_at(q, i, 1)
        wait_for(returned.at[target], r_recv.at[target])
    flat = returned[...].reshape(EXPERTS * UNIT, width)
    tokens = out_ref.shape[0]
    for c in range(SPLIT):
        both = jnp.dot(
            mix[c * 2 * tokens:(c + 1) * 2 * tokens, :], flat, preferred_element_type=jnp.float32
        )
        out_ref[:, c * width:(c + 1) * width] = (both[:tokens] + both[tokens:]).astype(jnp.bfloat16)
    for copy in sent:
        copy.wait_send()


def run_experts(normed, place, mix, w_gate, w_up, w_down, n):
    tokens, wide = normed.shape
    width = wide // SPLIT
    members = n // EXPERTS
    ff = w_gate.shape[1]
    chunk_rows = n * CAP // CHUNKS
    block = EXPERTS // CHUNKS
    tall = np.arange(PAIR * UNIT)
    column, rest = tall // (PAIR * CAP), tall % (PAIR * CAP)
    origin = (rest // CAP) * UNIT + column * CAP + rest % CAP
    perm = np.zeros((PAIR * UNIT, PAIR * UNIT), np.float32)
    perm[tall, origin] = 1.0
    order = jnp.asarray(perm, jnp.bfloat16)
    order_t = jnp.asarray(perm.T, jnp.bfloat16)
    vmem = pl.BlockSpec(memory_space=pltpu.VMEM)
    any_spec = pl.BlockSpec(memory_space=pl.ANY)
    bf16 = jnp.bfloat16
    dma = pltpu.SemaphoreType.DMA
    more = max(members - 1, 1)
    return pl.pallas_call(
        functools.partial(experts_kernel, n),
        out_shape=jax.ShapeDtypeStruct((tokens, wide), bf16),
        in_specs=[vmem] * 5 + [any_spec] * 3,
        out_specs=vmem,
        scratch_shapes=[
            pltpu.VMEM(w_gate.shape, bf16),
            pltpu.VMEM(w_up.shape, bf16),
            pltpu.VMEM(w_down.shape, bf16),
            pltpu.VMEM((EXPERTS, UNIT, width), bf16),
            pltpu.VMEM((n, UNIT, width), bf16),
            pltpu.VMEM((chunk_rows, wide), bf16),
            pltpu.VMEM((CHUNKS, chunk_rows, ff), bf16),
            pltpu.VMEM((CHUNKS, chunk_rows, ff), jnp.float32),
            pltpu.VMEM((CHUNKS, chunk_rows, ff), bf16),
            pltpu.VMEM((2, CHUNKS, chunk_rows, ff // 2), bf16),
            pltpu.VMEM((EXPERTS, members, UNIT, width), bf16),
            pltpu.VMEM((more, EXPERTS, UNIT, width), bf16),
            pltpu.VMEM((EXPERTS, UNIT, width), bf16),
            pltpu.VMEM((EXPERTS, UNIT, width), bf16),
            dma((3,)),
            dma((1,)),
            dma((EXPERTS,)),
            dma((EXPERTS, more)),
            dma((n,)),
            dma((CHUNKS,)),
            dma((CHUNKS,)),
            dma((CHUNKS,)),
            dma((CHUNKS,)),
            dma((CHUNKS, more)),
            dma((CHUNKS, more)),
            dma((EXPERTS,)),
            dma((EXPERTS,)),
        ],
        compiler_params=pltpu.CompilerParams(
            collective_id=1, has_side_effects=True, vmem_limit_bytes=60 << 20
        ),
        name="experts",
    )(normed, place, mix, order, order_t, w_gate, w_up, w_down)


def experts_by_kernel(normed, cells, combine, w_gate, w_up, w_down, n):
    tokens = normed.shape[0]
    unit = np.arange(EXPERTS * UNIT)
    cell = jnp.asarray((unit // UNIT) * CAP + unit % CAP, jnp.int32)
    column = jnp.asarray((unit % UNIT) // CAP, jnp.int32)
    split = jnp.arange(SPLIT, dtype=jnp.int32)
    same = column[:, None] == split[None, :]
    taken = (cells[:, 0][None, :] == cell[:, None]) | (cells[:, 1][None, :] == cell[:, None])
    place = (same[:, :, None] & taken[:, None, :]).astype(jnp.bfloat16)
    place = place.reshape(EXPERTS * UNIT, SPLIT * tokens)
    share = jnp.where(cells[:, 0][:, None] == cell[None, :], combine[:, 0][:, None], 0.0) + jnp.where(
        cells[:, 1][:, None] == cell[None, :], combine[:, 1][:, None], 0.0
    )
    coarse = share.astype(jnp.bfloat16)
    fine = (share - lax.reduce_precision(share, 8, 7)).astype(jnp.bfloat16)
    both = jnp.stack([coarse, fine])
    mix = jnp.where((split[:, None] == column[None, :])[:, None, None, :], both[None], 0)
    mix = mix.astype(jnp.bfloat16).reshape(SPLIT * 2 * tokens, EXPERTS * UNIT)
    return run_experts(normed, place, mix, w_gate, w_up, w_down, n)


def on_device(queries, keys, values, gain, router, w_gate, w_up, w_down, routes):
    cycle_size = lax.axis_size("ctx")
    token_count = queries.shape[0]
    attended = attend(queries, keys, values, cycle_size)
    attn_float = attended.astype(jnp.float32)
    gained = attn_float * gain[None, :]
    part_squares = jnp.sum(attn_float * attn_float, axis=1)
    part_logits = jnp.dot(gained, router, precision=lax.Precision.HIGHEST)
    squares, logits = lax.psum((part_squares, part_logits), "sec")
    factor = lax.rsqrt(squares / D + 1e-05)
    normed = (gained * factor[:, None]).astype(jnp.bfloat16)
    logits = logits * factor[:, None]
    expert_ids = jnp.arange(EXPERTS, dtype=jnp.int32)
    picks = (routes[:, :, None] == expert_ids[None, None, :]).astype(jnp.float32)
    chosen = jnp.sum(picks * logits[:, None, :], axis=2)
    combine = 1.0 / jnp.sum(jnp.exp(chosen[:, None, :] - chosen[:, :, None]), axis=2)
    flat_routes = routes.reshape(token_count * TOP)
    hot = (flat_routes[:, None] == expert_ids[None, :]).astype(jnp.int32)
    before = jnp.cumsum(hot, axis=0) - hot
    slots = jnp.sum(before * hot, axis=1)
    cells = flat_routes * CAP + slots
    if cycle_size * CAP <= 640:
        moe_out = experts_by_kernel(
            normed, cells.reshape(token_count, TOP), combine, w_gate, w_up, w_down, cycle_size
        )
        return (normed, moe_out)
    placing = (cells[:, None] == jnp.arange(EXPERTS * CAP, dtype=jnp.int32)[None, :]).astype(
        jnp.float32
    )
    placing = placing.reshape(token_count, TOP, EXPERTS * CAP)
    token_place = jnp.sum(placing, axis=1).astype(jnp.bfloat16)
    width_local = normed.shape[1]
    packed = jnp.einsum(
        "tc,td->cd", token_place, normed, preferred_element_type=jnp.float32
    ).astype(jnp.bfloat16)
    group_count = cycle_size // EXPERTS
    outgoing = jnp.broadcast_to(
        packed.reshape(EXPERTS, 1, CAP, width_local), (EXPERTS, group_count, CAP, width_local)
    )
    outgoing = outgoing.reshape(cycle_size, CAP, width_local)
    received = lax.all_to_all(outgoing, "ctx", split_axis=0, concat_axis=0, tiled=True)
    gate_part = jnp.einsum("sid,df->sif", received, w_gate, preferred_element_type=jnp.float32)
    up_part = jnp.einsum("sid,df->sif", received, w_up, preferred_element_type=jnp.float32)
    gate_full = lax.psum(gate_part.astype(jnp.bfloat16), "sec").astype(jnp.float32)
    up_full = lax.psum(up_part.astype(jnp.bfloat16), "sec").astype(jnp.float32)
    hidden = (jax.nn.silu(gate_full) * up_full).astype(jnp.bfloat16)
    down_part = jnp.einsum(
        "sif,fd->sid", hidden, w_down, preferred_element_type=jnp.float32
    ).astype(jnp.bfloat16)
    returned = lax.all_to_all(down_part, "ctx", split_axis=0, concat_axis=0, tiled=True)
    summed = jnp.sum(
        returned.reshape(EXPERTS, group_count, CAP, width_local).astype(jnp.float32), axis=1
    )
    summed = summed.reshape(EXPERTS * CAP, width_local)
    mixing = jnp.sum(placing * combine[:, :, None], axis=1)
    moe_out = jnp.dot(mixing, summed, precision=lax.Precision.HIGHEST).astype(jnp.bfloat16)
    return (normed, moe_out)


def solution(mesh):
    in_specs = (
        P("ctx", "sec"),
        P("ctx", "sec"),
        P("ctx", "sec"),
        P("sec"),
        P("sec", None),
        P("sec", "ctx"),
        P("sec", "ctx"),
        P("ctx", "sec"),
        P("ctx", None),
    )
    out_specs = (P("ctx", "sec"), P("ctx", "sec"))
    return jax.shard_map(
        on_device, mesh=mesh, in_specs=in_specs, out_specs=out_specs, check_vma=False
    )
```

```python
import functools
import math

import jax
import jax.numpy as jnp
import numpy as np
from jax import lax
from jax.experimental import pallas as pl
from jax.experimental.pallas import tpu as pltpu
from jax.sharding import PartitionSpec as P

D = 6144
HEADS = 48
KV_HEADS = 8
HEAD_DIM = 128
EXPERTS = 8
TOP = 2
CAP = 20
SPLIT = 4
UNIT = CAP * SPLIT
CHUNKS = 4
PAIR = 4
MESH = pl.DeviceIdType.MESH


def on_ctx(index):
    return {"ctx": index}


def attend_kernel(
    n, q_hbm, k_hbm, v_hbm, gain, router, normed, logits, q_ref, kv, q_rows, top, total, mixed, attended,
    stats, stats_in, local_sem, z_send, y_send, c_send, recv, s_send, s_recv,
):
    me, sec = lax.axis_index("ctx"), lax.axis_index("sec")
    far = n // 4
    zi, yi, ci = me // 4, (me // 2) % 2, me % 2
    rows = k_hbm.shape[0]

    def slot(source):
        return kv.at[:, pl.ds(pl.multiple_of(source * rows, 16), rows), :]

    mine = pl.ds(pl.multiple_of(me * rows, 16), rows)
    loads = [
        pltpu.make_async_copy(k_hbm, kv.at[0, mine, :], local_sem.at[0]),
        pltpu.make_async_copy(v_hbm, kv.at[1, mine, :], local_sem.at[1]),
        pltpu.make_async_copy(q_hbm, q_ref, local_sem.at[2]),
    ]
    for load in loads:
        load.start()
    y_peer = zi * 4 + (1 - yi) * 2 + ci
    c_peer = zi * 4 + yi * 2 + 1 - ci
    barrier = pltpu.get_barrier_semaphore()
    for k in range(1, far):
        pl.semaphore_signal(
            barrier, inc=1, device_id=on_ctx(((zi + k) % far) * 4 + yi * 2 + ci), device_id_type=MESH
        )
    for peer in (y_peer, c_peer):
        pl.semaphore_signal(barrier, inc=1, device_id=on_ctx(peer), device_id_type=MESH)
    pl.semaphore_signal(barrier, inc=1, device_id={"sec": 1 - sec}, device_id_type=MESH)
    pl.semaphore_wait(barrier, far + 2)
    loads[0].wait()
    loads[1].wait()
    sent = []

    def send(source, peer, sem):
        copy = pltpu.make_async_remote_copy(
            src_ref=slot(source), dst_ref=slot(source), send_sem=sem, recv_sem=recv.at[source],
            device_id=on_ctx(peer), device_id_type=MESH,
        )
        copy.start()
        sent.append(copy)

    def arrived(source):
        pltpu.make_async_remote_copy(
            src_ref=slot(source), dst_ref=slot(source), send_sem=c_send.at[0], recv_sem=recv.at[source],
            device_id=on_ctx(c_peer), device_id_type=MESH,
        ).wait_recv()

    tokens, wide = q_ref.shape
    group = HEADS // KV_HEADS
    heads = k_hbm.shape[1] // HEAD_DIM
    length = 4 * rows
    position = (rows - tokens) * n + me * tokens + lax.broadcasted_iota(jnp.int32, (tokens, length), 0)
    lane = lax.broadcasted_iota(jnp.int32, (tokens, length), 1)
    scale_factor = 1.0 / math.sqrt(HEAD_DIM)

    def attend_to(k):
        z = (zi + far - k) % far
        visible = (lane + z * length <= position)[None]
        span = pl.ds(pl.multiple_of(z * length, 16), length)

        def one_head(g, carry):
            at = pl.ds(pl.multiple_of(g * HEAD_DIM, HEAD_DIM), HEAD_DIM)
            scores = lax.dot_general(
                q_rows[g], kv[0, span, at], (((1,), (1,)), ((), ())), preferred_element_type=jnp.float32
            )
            scores = scores.reshape(group, tokens, length) * scale_factor
            scores = jnp.where(visible, scores, -1e30).reshape(group * tokens, length)
            newest = jnp.max(scores, axis=1, keepdims=True)
            if k > 0:
                newest = jnp.maximum(newest, top[g])
            w = jnp.exp(scores - newest)
            add = jnp.sum(w, axis=1, keepdims=True)
            out = jnp.dot(w.astype(jnp.bfloat16), kv[1, span, at], preferred_element_type=jnp.float32)
            if k > 0:
                fade = jnp.exp(top[g] - newest)
                add = add + fade * total[g]
                out = out + fade * mixed[g]
            top[g] = newest
            total[g] = add
            mixed[g] = out
            return carry

        lax.fori_loop(0, heads, one_head, 0)

    def z_forward(k):
        source = ((zi + far - k) % far) * 4 + yi * 2 + ci
        arrived(source)
        send(source, y_peer, y_send.at[k])
        send(source, c_peer, c_send.at[k])

    def y_forward(k):
        source = ((zi + far - k) % far) * 4 + (1 - yi) * 2 + ci
        arrived(source)
        send(source, c_peer, c_send.at[far + k])

    def c_wait(k):
        for y in range(2):
            arrived(((zi + far - k) % far) * 4 + y * 2 + 1 - ci)

    for k in range(1, far):
        send(me, ((zi + k) % far) * 4 + yi * 2 + ci, z_send.at[k - 1])
    send(me, y_peer, y_send.at[0])
    send(me, c_peer, c_send.at[0])
    loads[2].wait()
    for g in range(heads):
        for h in range(group):
            column = (g * group + h) * HEAD_DIM
            q_rows[g, h * tokens:(h + 1) * tokens, :] = q_ref[:, column:column + HEAD_DIM]
    y_forward(0)
    c_wait(0)
    for k in range(1, far):
        z_forward(k)
        attend_to(k - 1)
        y_forward(k)
        c_wait(k)
    attend_to(far - 1)

    squares = jnp.zeros((tokens, 1), jnp.float32)
    for g in range(heads):
        for h in range(group):
            column = (g * group + h) * HEAD_DIM
            part = slice(h * tokens, (h + 1) * tokens)
            out = (mixed[g, part, :] / total[g, part, :]).astype(jnp.bfloat16).astype(jnp.float32)
            squares = squares + jnp.sum(out * out, axis=1, keepdims=True)
            attended[:, column:column + HEAD_DIM] = out * gain[:, column:column + HEAD_DIM]
    stats[0] = jnp.zeros_like(stats[0])
    stats[0, :, :EXPERTS] = jnp.dot(
        attended[...], router[...], preferred_element_type=jnp.float32, precision=lax.Precision.HIGHEST
    )
    stats[1] = jnp.broadcast_to(squares, stats.shape[1:])
    swap = pltpu.make_async_remote_copy(
        src_ref=stats, dst_ref=stats_in, send_sem=s_send.at[0], recv_sem=s_recv.at[0],
        device_id={"sec": 1 - sec}, device_id_type=MESH,
    )
    swap.start()
    swap.wait()
    factor = lax.rsqrt((stats[1] + stats_in[1]) / D + 1e-05)
    logits[...] = (stats[0] + stats_in[0]) * factor
    normed[...] = (attended[...] * factor[:, :1]).astype(jnp.bfloat16)
    for copy in sent:
        copy.wait_send()


def attend(queries, keys, values, gain, router, n):
    rows, width = keys.shape
    tokens = queries.shape[0]
    group = HEADS // KV_HEADS
    heads = width // HEAD_DIM
    hbm = pl.BlockSpec(memory_space=pltpu.HBM)
    vmem = pl.BlockSpec(memory_space=pltpu.VMEM)
    f32 = jnp.float32
    return pl.pallas_call(
        functools.partial(attend_kernel, n),
        out_shape=(
            jax.ShapeDtypeStruct(queries.shape, jnp.bfloat16),
            jax.ShapeDtypeStruct((tokens, 128), f32),
        ),
        in_specs=[hbm] * 3 + [vmem] * 2,
        out_specs=(vmem, vmem),
        scratch_shapes=[
            pltpu.VMEM(queries.shape, jnp.bfloat16),
            pltpu.VMEM((2, n * rows, width), jnp.bfloat16),
            pltpu.VMEM((heads, group * tokens, HEAD_DIM), jnp.bfloat16),
            pltpu.VMEM((heads, group * tokens, 1), f32),
            pltpu.VMEM((heads, group * tokens, 1), f32),
            pltpu.VMEM((heads, group * tokens, HEAD_DIM), f32),
            pltpu.VMEM(queries.shape, f32),
            pltpu.VMEM((2, tokens, 128), f32),
            pltpu.VMEM((2, tokens, 128), f32),
            pltpu.SemaphoreType.DMA((3,)),
            pltpu.SemaphoreType.DMA((n // 4,)),
            pltpu.SemaphoreType.DMA((n // 4,)),
            pltpu.SemaphoreType.DMA((n // 2,)),
            pltpu.SemaphoreType.DMA((n,)),
            pltpu.SemaphoreType.DMA((1,)),
            pltpu.SemaphoreType.DMA((1,)),
        ],
        compiler_params=pltpu.CompilerParams(
            collective_id=0, has_side_effects=True, vmem_limit_bytes=48 << 20
        ),
        name="attend",
    )(queries, keys, values, gain.reshape(1, -1), router)


def experts_kernel(
    n, normed, logits, routes, order, order_t, w_gate, w_up, w_down, out_ref,
    mix, gate_w, up_w, down_w, packed, disp, rows_x, gu_send, gu_own, gu_recv, hidden, parts, group_parts,
    back, returned, w_sem, own_sem, d_send, f_send, d_recv, x_send, x_recv, h_send, h_recv,
    g_send, g_recv, r_send, r_recv,
):
    me, sec = lax.axis_index("ctx"), lax.axis_index("sec")
    members = n // EXPERTS
    block = EXPERTS // CHUNKS
    e, j = me // members, me % members
    b, el = e // block, e % block
    width = packed.shape[2]
    half = gate_w.shape[1] // 2
    chunk_rows = block * members * CAP
    tile = 256

    loads = [
        pltpu.make_async_copy(w_gate, gate_w, w_sem.at[0]),
        pltpu.make_async_copy(w_up, up_w, w_sem.at[1]),
        pltpu.make_async_copy(w_down, down_w, w_sem.at[2]),
    ]
    for load in loads:
        load.start()

    def block_at(q):
        pair = (b // 2 + 1) % 2 if q < 2 else b // 2
        return pair * 2 + (b % 2 if q % 2 == (0 if q < 2 else 1) else 1 - b % 2)

    def expert_at(q, i, sign):
        return block_at(q) * block + (el + block + sign * i) % block

    last = (CHUNKS - 1, 0)
    others = [(q, i) for q in range(CHUNKS) for i in range(block) if (q, i) != last]
    barrier = pltpu.get_barrier_semaphore()
    for q, i in others:
        pl.semaphore_signal(
            barrier, inc=1, device_id=on_ctx(expert_at(q, i, 1) * members + j), device_id_type=MESH
        )
    for g in range(1, members):
        pl.semaphore_signal(
            barrier, inc=1, device_id=on_ctx(e * members + (j + g) % members), device_id_type=MESH
        )
    pl.semaphore_signal(barrier, inc=1, device_id={"sec": 1 - sec}, device_id_type=MESH)

    tokens = normed.shape[0]
    f32 = jnp.float32
    lane = lax.broadcasted_iota(jnp.int32, (tokens, 128), 1)
    picks = [(lane == routes[:, k:k + 1]).astype(f32) for k in range(TOP)]
    earlier = (
        lax.broadcasted_iota(jnp.int32, (tokens, tokens), 1) < lax.broadcasted_iota(jnp.int32, (tokens, tokens), 0)
    )
    before = jnp.dot(
        earlier.astype(jnp.bfloat16), (picks[0] + picks[1]).astype(jnp.bfloat16), preferred_element_type=f32
    )
    chosen = [jnp.sum(pick * logits[...], axis=1, keepdims=True) for pick in picks]
    cells = [
        routes[:, k:k + 1].astype(f32) * CAP + jnp.sum(picks[k] * before, axis=1, keepdims=True)
        for k in range(TOP)
    ]
    combine = [1.0 / (1.0 + jnp.exp(chosen[1 - k] - chosen[k])) for k in range(TOP)]
    spot = lax.broadcasted_iota(jnp.int32, (tokens, EXPERTS * UNIT), 1)
    unit = (spot * 820) >> 16
    rest = spot - unit * UNIT
    column = (rest * 3277) >> 16
    cell = (unit * CAP + rest - column * CAP).astype(f32)
    hits = [cell == cells[k] for k in range(TOP)]
    placing = jnp.where(hits[0] | hits[1], 1.0, 0.0)
    share = jnp.where(hits[0], combine[0], 0.0) + jnp.where(hits[1], combine[1], 0.0)
    coarse = share.astype(jnp.bfloat16).astype(f32)
    fine = share - coarse
    place = jnp.concatenate([jnp.where(column == c, placing, 0.0) for c in range(SPLIT)], axis=0)
    for c in range(SPLIT):
        mix[2 * c * tokens:(2 * c + 1) * tokens, :] = jnp.where(column == c, coarse, 0.0).astype(jnp.bfloat16)
        mix[(2 * c + 1) * tokens:(2 * c + 2) * tokens, :] = jnp.where(column == c, fine, 0.0).astype(jnp.bfloat16)
    stacked = jnp.concatenate([normed[:, c * width:(c + 1) * width] for c in range(SPLIT)], axis=0)
    rows_out = lax.dot_general(
        place.astype(jnp.bfloat16), stacked, (((0,), (0,)), ((), ())), preferred_element_type=f32
    ).astype(jnp.bfloat16)
    for x in range(EXPERTS):
        packed[x] = rows_out[x * UNIT:(x + 1) * UNIT]
    pl.semaphore_wait(barrier, EXPERTS - 1 + members)

    sent = []

    def remote(src, dst, send_sem, recv_sem, device):
        return pltpu.make_async_remote_copy(
            src_ref=src, dst_ref=dst, send_sem=send_sem, recv_sem=recv_sem,
            device_id=device, device_id_type=MESH,
        )

    def send(src, dst, send_sem, recv_sem, device):
        copy = remote(src, dst, send_sem, recv_sem, device)
        copy.start()
        sent.append(copy)

    def wait_for(dst, recv_sem):
        remote(dst, dst, d_send.at[0], recv_sem, {"sec": 1 - sec}).wait_recv()

    for number, (q, i) in enumerate(others):
        target = expert_at(q, i, 1)
        send(packed.at[target], disp.at[me], d_send.at[number], d_recv.at[me], on_ctx(target * members + j))
    own = pltpu.make_async_copy(packed.at[e], disp.at[me], own_sem.at[0])
    own.start()
    for g in range(1, members):
        send(
            packed.at[e], disp.at[me], f_send.at[0, g - 1], d_recv.at[me],
            on_ctx(e * members + (j + g) % members),
        )

    def first_slot(q):
        return block_at(q) * block * members

    def forward(q):
        for i in range(block):
            if (q, i) == last:
                continue
            source = expert_at(q, i, -1) * members + j
            wait_for(disp.at[source], d_recv.at[source])
            for g in range(1, members):
                send(
                    disp.at[source], disp.at[source], f_send.at[q * block + i, g - 1], d_recv.at[source],
                    on_ctx(e * members + (j + g) % members),
                )

    def gate_up(q):
        if q == CHUNKS - 1:
            own.wait()
        for i in range(block):
            for g in range(1, members):
                source = expert_at(q, i, -1) * members + (j + g) % members
                wait_for(disp.at[source], d_recv.at[source])
        first = first_slot(q)
        for u in range(block * members // PAIR):
            flat = disp[pl.ds(first + u * PAIR, PAIR)].reshape(PAIR * UNIT, width)
            tall = jnp.dot(order[...], flat, preferred_element_type=jnp.float32).astype(jnp.bfloat16)
            for c in range(SPLIT):
                rows_x[u * PAIR * CAP:(u + 1) * PAIR * CAP, c * width:(c + 1) * width] = tall[
                    c * PAIR * CAP:(c + 1) * PAIR * CAP
                ]
        if q == 0:
            loads[0].wait()
            loads[1].wait()

        def product(weights, base, t):
            at = pl.ds(pl.multiple_of(base + t * tile, tile), tile)
            return jnp.dot(rows_x[...], weights[:, at], preferred_element_type=jnp.float32)

        def peers(t, carry):
            at = pl.multiple_of(t * tile, tile)
            gu_send[q, :, pl.ds(at, tile)] = product(gate_w, (1 - sec) * half, t).astype(jnp.bfloat16)
            gu_send[q, :, pl.ds(at + half, tile)] = product(up_w, (1 - sec) * half, t).astype(jnp.bfloat16)
            return carry

        def mine(t, carry):
            at = pl.multiple_of(t * tile, tile)
            gu_own[q, :, pl.ds(at, tile)] = product(gate_w, sec * half, t)
            gu_own[q, :, pl.ds(at + half, tile)] = product(up_w, sec * half, t)
            return carry

        lax.fori_loop(0, half // tile, peers, 0)
        send(gu_send.at[q], gu_recv.at[q], x_send.at[q], x_recv.at[q], {"sec": 1 - sec})
        lax.fori_loop(0, half // tile, mine, 0)

    def activate(q):
        wait_for(gu_recv.at[q], x_recv.at[q])
        full = gu_own[q] + gu_recv[q].astype(jnp.float32)
        gate, up = full[:, :half], full[:, half:]
        hidden[sec, q] = (gate / (1.0 + jnp.exp(-gate)) * up).astype(jnp.bfloat16)
        send(hidden.at[sec, q], hidden.at[sec, q], h_send.at[q], h_recv.at[q], {"sec": 1 - sec})

    def down(q):
        wait_for(hidden.at[1 - sec, q], h_recv.at[q])
        if q == 0:
            loads[2].wait()
        first = first_slot(q)
        both = jnp.concatenate([hidden[0, q], hidden[1, q]], axis=1)
        wide = [
            jnp.dot(both, down_w[:, c * width:(c + 1) * width], preferred_element_type=jnp.float32).astype(
                jnp.bfloat16
            )
            for c in range(SPLIT)
        ]
        for u in range(block * members // PAIR):
            tall = jnp.concatenate([w[u * PAIR * CAP:(u + 1) * PAIR * CAP] for w in wide], axis=0)
            flat = jnp.dot(order_t[...], tall, preferred_element_type=jnp.float32).astype(jnp.bfloat16)
            for s in range(PAIR):
                at = first + u * PAIR + s
                parts[at // members, at % members] = flat[s * UNIT:(s + 1) * UNIT]
        start = first // members
        for g in range(1, members):
            to = (j + g) % members
            send(
                parts.at[pl.ds(start, block), to], group_parts.at[g - 1, pl.ds(start, block)],
                g_send.at[q, g - 1], g_recv.at[q, g - 1], on_ctx(e * members + to),
            )

    def give_back(q):
        start = first_slot(q) // members
        for g in range(1, members):
            wait_for(group_parts.at[g - 1, pl.ds(start, block)], g_recv.at[q, g - 1])
        for i in range(block):
            source = expert_at(q, i, -1)
            total = parts[source, j].astype(jnp.float32)
            for g in range(1, members):
                total = total + group_parts[g - 1, source].astype(jnp.float32)
            if (q, i) == last:
                returned[e] = total.astype(jnp.bfloat16)
            else:
                back[source] = total.astype(jnp.bfloat16)
                send(
                    back.at[source], returned.at[e], r_send.at[q * block + i], r_recv.at[e],
                    on_ctx(source * members + j),
                )

    stages = (forward, gate_up, activate, down, give_back)
    lag = (0, 0, 1, 1, 2)
    for step in range(CHUNKS + max(lag)):
        for stage, delay in sorted(zip(stages, lag), key=lambda pair: pair[1]):
            if 0 <= step - delay < CHUNKS:
                stage(step - delay)

    for q, i in others:
        target = expert_at(q, i, 1)
        wait_for(returned.at[target], r_recv.at[target])
    flat = returned[...].reshape(EXPERTS * UNIT, width)
    for c in range(SPLIT):
        both = jnp.dot(
            mix[c * 2 * tokens:(c + 1) * 2 * tokens, :], flat, preferred_element_type=jnp.float32
        )
        out_ref[:, c * width:(c + 1) * width] = (both[:tokens] + both[tokens:]).astype(jnp.bfloat16)
    for copy in sent:
        copy.wait_send()


def run_experts(normed, logits, routes, w_gate, w_up, w_down, n):
    tokens, wide = normed.shape
    width = wide // SPLIT
    members = n // EXPERTS
    ff = w_gate.shape[1]
    chunk_rows = n * CAP // CHUNKS
    block = EXPERTS // CHUNKS
    tall = np.arange(PAIR * UNIT)
    column, rest = tall // (PAIR * CAP), tall % (PAIR * CAP)
    origin = (rest // CAP) * UNIT + column * CAP + rest % CAP
    perm = np.zeros((PAIR * UNIT, PAIR * UNIT), np.float32)
    perm[tall, origin] = 1.0
    order = jnp.asarray(perm, jnp.bfloat16)
    order_t = jnp.asarray(perm.T, jnp.bfloat16)
    vmem = pl.BlockSpec(memory_space=pltpu.VMEM)
    any_spec = pl.BlockSpec(memory_space=pltpu.HBM)
    bf16 = jnp.bfloat16
    dma = pltpu.SemaphoreType.DMA
    more = max(members - 1, 1)
    return pl.pallas_call(
        functools.partial(experts_kernel, n),
        out_shape=jax.ShapeDtypeStruct((tokens, wide), bf16),
        in_specs=[vmem] * 5 + [any_spec] * 3,
        out_specs=vmem,
        scratch_shapes=[
            pltpu.VMEM((SPLIT * 2 * tokens, EXPERTS * UNIT), bf16),
            pltpu.VMEM(w_gate.shape, bf16),
            pltpu.VMEM(w_up.shape, bf16),
            pltpu.VMEM(w_down.shape, bf16),
            pltpu.VMEM((EXPERTS, UNIT, width), bf16),
            pltpu.VMEM((n, UNIT, width), bf16),
            pltpu.VMEM((chunk_rows, wide), bf16),
            pltpu.VMEM((CHUNKS, chunk_rows, ff), bf16),
            pltpu.VMEM((CHUNKS, chunk_rows, ff), jnp.float32),
            pltpu.VMEM((CHUNKS, chunk_rows, ff), bf16),
            pltpu.VMEM((2, CHUNKS, chunk_rows, ff // 2), bf16),
            pltpu.VMEM((EXPERTS, members, UNIT, width), bf16),
            pltpu.VMEM((more, EXPERTS, UNIT, width), bf16),
            pltpu.VMEM((EXPERTS, UNIT, width), bf16),
            pltpu.VMEM((EXPERTS, UNIT, width), bf16),
            dma((3,)),
            dma((1,)),
            dma((EXPERTS,)),
            dma((EXPERTS, more)),
            dma((n,)),
            dma((CHUNKS,)),
            dma((CHUNKS,)),
            dma((CHUNKS,)),
            dma((CHUNKS,)),
            dma((CHUNKS, more)),
            dma((CHUNKS, more)),
            dma((EXPERTS,)),
            dma((EXPERTS,)),
        ],
        compiler_params=pltpu.CompilerParams(
            collective_id=1, has_side_effects=True, vmem_limit_bytes=60 << 20
        ),
        name="experts",
    )(normed, logits, routes, order, order_t, w_gate, w_up, w_down)


def on_device(queries, keys, values, gain, router, w_gate, w_up, w_down, routes):
    cycle_size = lax.axis_size("ctx")
    token_count = queries.shape[0]
    normed, logits = attend(queries, keys, values, gain, router, cycle_size)
    if cycle_size * CAP <= 640:
        return (normed, run_experts(normed, logits, routes, w_gate, w_up, w_down, cycle_size))
    logits = logits[:, :EXPERTS]
    expert_ids = jnp.arange(EXPERTS, dtype=jnp.int32)
    picks = (routes[:, :, None] == expert_ids[None, None, :]).astype(jnp.float32)
    chosen = jnp.sum(picks * logits[:, None, :], axis=2)
    combine = 1.0 / jnp.sum(jnp.exp(chosen[:, None, :] - chosen[:, :, None]), axis=2)
    flat_routes = routes.reshape(token_count * TOP)
    hot = (flat_routes[:, None] == expert_ids[None, :]).astype(jnp.int32)
    before = jnp.cumsum(hot, axis=0) - hot
    slots = jnp.sum(before * hot, axis=1)
    cells = flat_routes * CAP + slots
    placing = (cells[:, None] == jnp.arange(EXPERTS * CAP, dtype=jnp.int32)[None, :]).astype(
        jnp.float32
    )
    placing = placing.reshape(token_count, TOP, EXPERTS * CAP)
    token_place = jnp.sum(placing, axis=1).astype(jnp.bfloat16)
    width_local = normed.shape[1]
    packed = jnp.einsum(
        "tc,td->cd", token_place, normed, preferred_element_type=jnp.float32
    ).astype(jnp.bfloat16)
    group_count = cycle_size // EXPERTS
    outgoing = jnp.broadcast_to(
        packed.reshape(EXPERTS, 1, CAP, width_local), (EXPERTS, group_count, CAP, width_local)
    )
    outgoing = outgoing.reshape(cycle_size, CAP, width_local)
    received = lax.all_to_all(outgoing, "ctx", split_axis=0, concat_axis=0, tiled=True)
    gate_part = jnp.einsum("sid,df->sif", received, w_gate, preferred_element_type=jnp.float32)
    up_part = jnp.einsum("sid,df->sif", received, w_up, preferred_element_type=jnp.float32)
    gate_full = lax.psum(gate_part.astype(jnp.bfloat16), "sec").astype(jnp.float32)
    up_full = lax.psum(up_part.astype(jnp.bfloat16), "sec").astype(jnp.float32)
    hidden = (jax.nn.silu(gate_full) * up_full).astype(jnp.bfloat16)
    down_part = jnp.einsum(
        "sif,fd->sid", hidden, w_down, preferred_element_type=jnp.float32
    ).astype(jnp.bfloat16)
    returned = lax.all_to_all(down_part, "ctx", split_axis=0, concat_axis=0, tiled=True)
    summed = jnp.sum(
        returned.reshape(EXPERTS, group_count, CAP, width_local).astype(jnp.float32), axis=1
    )
    summed = summed.reshape(EXPERTS * CAP, width_local)
    mixing = jnp.sum(placing * combine[:, :, None], axis=1)
    moe_out = jnp.dot(mixing, summed, precision=lax.Precision.HIGHEST).astype(jnp.bfloat16)
    return (normed, moe_out)


def solution(mesh):
    in_specs = (
        P("ctx", "sec"),
        P("ctx", "sec"),
        P("ctx", "sec"),
        P("sec"),
        P("sec", None),
        P("sec", "ctx"),
        P("sec", "ctx"),
        P("ctx", "sec"),
        P("ctx", None),
    )
    out_specs = (P("ctx", "sec"), P("ctx", "sec"))
    return jax.shard_map(
        on_device, mesh=mesh, in_specs=in_specs, out_specs=out_specs, check_vma=False
    )
```

```python
import functools
import math

import jax
import jax.numpy as jnp
from jax import lax
from jax.experimental import pallas as pl
from jax.experimental.pallas import tpu as pltpu
from jax.sharding import PartitionSpec as P

D = 6144
HEADS = 48
KV_HEADS = 8
HEAD_DIM = 128
EXPERTS = 8
TOP = 2
CAP = 20
SPLIT = 4
UNIT = CAP * SPLIT
CHUNKS = 2
PAIR = 4
MESH = pl.DeviceIdType.MESH


def on_ctx(index):
    return {"ctx": index}


def attend_kernel(
    n, q_hbm, k_hbm, v_hbm, gain, router, normed, logits, q_ref, kv, q_rows, top, total, mixed, attended,
    stats, stats_in, local_sem, z_send, y_send, c_send, recv, s_send, s_recv,
):
    me, sec = lax.axis_index("ctx"), lax.axis_index("sec")
    far = n // 4
    zi, yi, ci = me // 4, (me // 2) % 2, me % 2
    rows = k_hbm.shape[0]

    def slot(source):
        return kv.at[:, pl.ds(pl.multiple_of(source * rows, 16), rows), :]

    mine = pl.ds(pl.multiple_of(me * rows, 16), rows)
    loads = [
        pltpu.make_async_copy(k_hbm, kv.at[0, mine, :], local_sem.at[0]),
        pltpu.make_async_copy(v_hbm, kv.at[1, mine, :], local_sem.at[1]),
        pltpu.make_async_copy(q_hbm, q_ref, local_sem.at[2]),
    ]
    for load in loads:
        load.start()
    y_peer = zi * 4 + (1 - yi) * 2 + ci
    c_peer = zi * 4 + yi * 2 + 1 - ci
    barrier = pltpu.get_barrier_semaphore()
    for k in range(1, far):
        pl.semaphore_signal(
            barrier, inc=1, device_id=on_ctx(((zi + k) % far) * 4 + yi * 2 + ci), device_id_type=MESH
        )
    for peer in (y_peer, c_peer):
        pl.semaphore_signal(barrier, inc=1, device_id=on_ctx(peer), device_id_type=MESH)
    pl.semaphore_signal(barrier, inc=1, device_id={"sec": 1 - sec}, device_id_type=MESH)
    pl.semaphore_wait(barrier, far + 2)
    loads[0].wait()
    loads[1].wait()
    sent = []

    def send(source, peer, sem):
        copy = pltpu.make_async_remote_copy(
            src_ref=slot(source), dst_ref=slot(source), send_sem=sem, recv_sem=recv.at[source],
            device_id=on_ctx(peer), device_id_type=MESH,
        )
        copy.start()
        sent.append(copy)

    def arrived(source):
        pltpu.make_async_remote_copy(
            src_ref=slot(source), dst_ref=slot(source), send_sem=c_send.at[0], recv_sem=recv.at[source],
            device_id=on_ctx(c_peer), device_id_type=MESH,
        ).wait_recv()

    tokens, wide = q_ref.shape
    group = HEADS // KV_HEADS
    heads = k_hbm.shape[1] // HEAD_DIM
    length = 4 * rows
    position = (rows - tokens) * n + me * tokens + lax.broadcasted_iota(jnp.int32, (tokens, length), 0)
    lane = lax.broadcasted_iota(jnp.int32, (tokens, length), 1)
    scale_factor = 1.0 / math.sqrt(HEAD_DIM)

    def attend_to(k):
        z = (zi + far - k) % far
        visible = (lane + z * length <= position)[None]
        span = pl.ds(pl.multiple_of(z * length, 16), length)

        def one_head(g, carry):
            at = pl.ds(pl.multiple_of(g * HEAD_DIM, HEAD_DIM), HEAD_DIM)
            scores = lax.dot_general(
                q_rows[g], kv[0, span, at], (((1,), (1,)), ((), ())), preferred_element_type=jnp.float32
            )
            scores = scores.reshape(group, tokens, length) * scale_factor
            scores = jnp.where(visible, scores, -1e30).reshape(group * tokens, length)
            newest = jnp.max(scores, axis=1, keepdims=True)
            if k > 0:
                newest = jnp.maximum(newest, top[g])
            w = jnp.exp(scores - newest)
            add = jnp.sum(w, axis=1, keepdims=True)
            out = jnp.dot(w.astype(jnp.bfloat16), kv[1, span, at], preferred_element_type=jnp.float32)
            if k > 0:
                fade = jnp.exp(top[g] - newest)
                add = add + fade * total[g]
                out = out + fade * mixed[g]
            top[g] = newest
            total[g] = add
            mixed[g] = out
            return carry

        lax.fori_loop(0, heads, one_head, 0)

    def z_forward(k):
        source = ((zi + far - k) % far) * 4 + yi * 2 + ci
        arrived(source)
        send(source, y_peer, y_send.at[k])
        send(source, c_peer, c_send.at[k])

    def y_forward(k):
        source = ((zi + far - k) % far) * 4 + (1 - yi) * 2 + ci
        arrived(source)
        send(source, c_peer, c_send.at[far + k])

    def c_wait(k):
        for y in range(2):
            arrived(((zi + far - k) % far) * 4 + y * 2 + 1 - ci)

    for k in range(1, far):
        send(me, ((zi + k) % far) * 4 + yi * 2 + ci, z_send.at[k - 1])
    send(me, y_peer, y_send.at[0])
    send(me, c_peer, c_send.at[0])
    loads[2].wait()
    for g in range(heads):
        for h in range(group):
            column = (g * group + h) * HEAD_DIM
            q_rows[g, h * tokens:(h + 1) * tokens, :] = q_ref[:, column:column + HEAD_DIM]
    y_forward(0)
    c_wait(0)
    for k in range(1, far):
        z_forward(k)
    attend_to(0)
    for k in range(1, far):
        y_forward(k)
        c_wait(k)
        if k < far - 1:
            attend_to(k)
    attend_to(far - 1)

    squares = jnp.zeros((tokens, 1), jnp.float32)
    for g in range(heads):
        for h in range(group):
            column = (g * group + h) * HEAD_DIM
            part = slice(h * tokens, (h + 1) * tokens)
            out = (mixed[g, part, :] / total[g, part, :]).astype(jnp.bfloat16).astype(jnp.float32)
            squares = squares + jnp.sum(out * out, axis=1, keepdims=True)
            attended[:, column:column + HEAD_DIM] = out * gain[:, column:column + HEAD_DIM]
    stats[0] = jnp.zeros_like(stats[0])
    stats[0, :, :EXPERTS] = lax.dot_general(
        attended[...], router[...], (((1,), (1,)), ((), ())), preferred_element_type=jnp.float32,
        precision=lax.Precision.HIGHEST,
    )
    stats[1] = jnp.broadcast_to(squares, stats.shape[1:])
    swap = pltpu.make_async_remote_copy(
        src_ref=stats, dst_ref=stats_in, send_sem=s_send.at[0], recv_sem=s_recv.at[0],
        device_id={"sec": 1 - sec}, device_id_type=MESH,
    )
    swap.start()
    swap.wait()
    factor = lax.rsqrt((stats[1] + stats_in[1]) / D + 1e-05)
    logits[...] = (stats[0] + stats_in[0]) * factor
    normed[...] = (attended[...] * factor[:, :1]).astype(jnp.bfloat16)
    for copy in sent:
        copy.wait_send()


def attend(queries, keys, values, gain, router, n):
    rows, width = keys.shape
    tokens = queries.shape[0]
    group = HEADS // KV_HEADS
    heads = width // HEAD_DIM
    hbm = pl.BlockSpec(memory_space=pltpu.HBM)
    vmem = pl.BlockSpec(memory_space=pltpu.VMEM)
    f32 = jnp.float32
    return pl.pallas_call(
        functools.partial(attend_kernel, n),
        out_shape=(
            jax.ShapeDtypeStruct(queries.shape, jnp.bfloat16),
            jax.ShapeDtypeStruct((tokens, 128), f32),
        ),
        in_specs=[hbm] * 3 + [vmem] * 2,
        out_specs=(vmem, vmem),
        scratch_shapes=[
            pltpu.VMEM(queries.shape, jnp.bfloat16),
            pltpu.VMEM((2, n * rows, width), jnp.bfloat16),
            pltpu.VMEM((heads, group * tokens, HEAD_DIM), jnp.bfloat16),
            pltpu.VMEM((heads, group * tokens, 1), f32),
            pltpu.VMEM((heads, group * tokens, 1), f32),
            pltpu.VMEM((heads, group * tokens, HEAD_DIM), f32),
            pltpu.VMEM(queries.shape, f32),
            pltpu.VMEM((2, tokens, 128), f32),
            pltpu.VMEM((2, tokens, 128), f32),
            pltpu.SemaphoreType.DMA((3,)),
            pltpu.SemaphoreType.DMA((n // 4,)),
            pltpu.SemaphoreType.DMA((n // 4,)),
            pltpu.SemaphoreType.DMA((n // 2,)),
            pltpu.SemaphoreType.DMA((n,)),
            pltpu.SemaphoreType.DMA((1,)),
            pltpu.SemaphoreType.DMA((1,)),
        ],
        compiler_params=pltpu.CompilerParams(
            collective_id=0, has_side_effects=True, vmem_limit_bytes=63 << 20
        ),
        name="attend",
    )(queries, keys, values, gain.reshape(1, -1), router.T)


def experts_kernel(
    n, normed, logits, routes, w_gate, w_up, w_down, out_ref,
    order, order_t, mix, gate_w, up_w, down_w, packed, disp, rows_x, gu_send, gu_own, gu_recv, hidden, parts, group_parts,
    back, returned, w_sem, own_sem, d_send, f_send, d_recv, x_send, x_recv, h_send, h_recv,
    g_send, g_recv, r_send, r_recv,
):
    me, sec = lax.axis_index("ctx"), lax.axis_index("sec")
    members = n // EXPERTS
    block = EXPERTS // CHUNKS
    e, j = me // members, me % members
    b, el = e // block, e % block
    width = packed.shape[2]
    half = gate_w.shape[1] // 2
    chunk_rows = block * members * CAP
    tile = 256

    loads = [
        pltpu.make_async_copy(w_gate, gate_w, w_sem.at[0]),
        pltpu.make_async_copy(w_up, up_w, w_sem.at[1]),
        pltpu.make_async_copy(w_down, down_w, w_sem.at[2]),
    ]
    for load in loads:
        load.start()

    def block_at(q):
        return (b + 1 + q) % 2

    def expert_at(q, i, sign):
        return block_at(q) * block + (el + block + sign * i) % block

    last = (CHUNKS - 1, 0)
    others = [(q, i) for q in range(CHUNKS) for i in range(block) if (q, i) != last]
    barrier = pltpu.get_barrier_semaphore()
    for q, i in others:
        pl.semaphore_signal(
            barrier, inc=1, device_id=on_ctx(expert_at(q, i, 1) * members + j), device_id_type=MESH
        )
    for g in range(1, members):
        pl.semaphore_signal(
            barrier, inc=1, device_id=on_ctx(e * members + (j + g) % members), device_id_type=MESH
        )
    pl.semaphore_signal(barrier, inc=1, device_id={"sec": 1 - sec}, device_id_type=MESH)

    tokens = normed.shape[0]
    f32 = jnp.float32
    lane = lax.broadcasted_iota(jnp.int32, (tokens, 128), 1)
    down_at = lax.broadcasted_iota(jnp.int32, (tokens, tokens), 0)
    across_at = lax.broadcasted_iota(jnp.int32, (tokens, tokens), 1)
    named = lax.dot_general(
        (down_at == across_at).astype(jnp.bfloat16), routes[...].astype(f32).astype(jnp.bfloat16),
        (((1,), (1,)), ((), ())), preferred_element_type=f32,
    )
    picks = [(lane.astype(f32) == named[:, k:k + 1]).astype(f32) for k in range(TOP)]
    earlier = across_at < down_at
    before = jnp.dot(
        earlier.astype(jnp.bfloat16), (picks[0] + picks[1]).astype(jnp.bfloat16), preferred_element_type=f32
    )
    chosen = [jnp.sum(pick * logits[...], axis=1, keepdims=True) for pick in picks]
    cells = [
        named[:, k:k + 1] * CAP + jnp.sum(picks[k] * before, axis=1, keepdims=True)
        for k in range(TOP)
    ]
    combine = [1.0 / (1.0 + jnp.exp(chosen[1 - k] - chosen[k])) for k in range(TOP)]
    spot = lax.broadcasted_iota(jnp.int32, (tokens, EXPERTS * UNIT), 1)
    unit = (spot * 820) >> 16
    rest = spot - unit * UNIT
    column = (rest * 3277) >> 16
    cell = (unit * CAP + rest - column * CAP).astype(f32)
    hits = [cell == cells[k] for k in range(TOP)]
    placing = jnp.where(hits[0] | hits[1], 1.0, 0.0)
    place = jnp.concatenate([jnp.where(column == c, placing, 0.0) for c in range(SPLIT)], axis=0)
    stacked = jnp.concatenate([normed[:, c * width:(c + 1) * width] for c in range(SPLIT)], axis=0)
    rows_out = lax.dot_general(
        place.astype(jnp.bfloat16), stacked, (((0,), (0,)), ((), ())), preferred_element_type=f32
    ).astype(jnp.bfloat16)
    for x in range(EXPERTS):
        packed[x] = rows_out[x * UNIT:(x + 1) * UNIT]
    pl.semaphore_wait(barrier, EXPERTS - 1 + members)

    sent = []

    def remote(src, dst, send_sem, recv_sem, device):
        return pltpu.make_async_remote_copy(
            src_ref=src, dst_ref=dst, send_sem=send_sem, recv_sem=recv_sem,
            device_id=device, device_id_type=MESH,
        )

    def send(src, dst, send_sem, recv_sem, device):
        copy = remote(src, dst, send_sem, recv_sem, device)
        copy.start()
        sent.append(copy)

    def wait_for(dst, recv_sem):
        remote(dst, dst, d_send.at[0], recv_sem, {"sec": 1 - sec}).wait_recv()

    for number, (q, i) in enumerate(others):
        target = expert_at(q, i, 1)
        send(packed.at[target], disp.at[me], d_send.at[number], d_recv.at[me], on_ctx(target * members + j))
    own = pltpu.make_async_copy(packed.at[e], disp.at[me], own_sem.at[0])
    own.start()
    for g in range(1, members):
        send(
            packed.at[e], disp.at[me], f_send.at[0, g - 1], d_recv.at[me],
            on_ctx(e * members + (j + g) % members),
        )

    share = jnp.where(hits[0], combine[0], 0.0) + jnp.where(hits[1], combine[1], 0.0)
    coarse = share.astype(jnp.bfloat16).astype(f32)
    fine = share - coarse
    for c in range(SPLIT):
        mix[2 * c * tokens:(2 * c + 1) * tokens, :] = jnp.where(column == c, coarse, 0.0).astype(jnp.bfloat16)
        mix[(2 * c + 1) * tokens:(2 * c + 2) * tokens, :] = jnp.where(column == c, fine, 0.0).astype(jnp.bfloat16)

    side = PAIR * UNIT

    def origin(spot):
        split = (spot * 820) >> 16
        rest = spot - split * UNIT
        source = (rest * 3277) >> 16
        return source * UNIT + split * CAP + rest - source * CAP

    rows_at = lax.broadcasted_iota(jnp.int32, (side, side), 0)
    columns_at = lax.broadcasted_iota(jnp.int32, (side, side), 1)
    order[...] = jnp.where(columns_at == origin(rows_at), 1.0, 0.0).astype(jnp.bfloat16)
    order_t[...] = jnp.where(rows_at == origin(columns_at), 1.0, 0.0).astype(jnp.bfloat16)

    def first_slot(q):
        return block_at(q) * block * members

    def forward(q):
        for i in range(block):
            if (q, i) == last:
                continue
            source = expert_at(q, i, -1) * members + j
            wait_for(disp.at[source], d_recv.at[source])
            for g in range(1, members):
                send(
                    disp.at[source], disp.at[source], f_send.at[q * block + i, g - 1], d_recv.at[source],
                    on_ctx(e * members + (j + g) % members),
                )

    def gate_up(q):
        if q == CHUNKS - 1:
            own.wait()
        for i in range(block):
            for g in range(1, members):
                source = expert_at(q, i, -1) * members + (j + g) % members
                wait_for(disp.at[source], d_recv.at[source])
        first = first_slot(q)
        for u in range(block * members // PAIR):
            flat = disp[pl.ds(first + u * PAIR, PAIR)].reshape(PAIR * UNIT, width)
            tall = jnp.dot(order[...], flat, preferred_element_type=jnp.float32).astype(jnp.bfloat16)
            for c in range(SPLIT):
                rows_x[u * PAIR * CAP:(u + 1) * PAIR * CAP, c * width:(c + 1) * width] = tall[
                    c * PAIR * CAP:(c + 1) * PAIR * CAP
                ]
        if q == 0:
            loads[0].wait()
            loads[1].wait()

        def product(weights, base, t):
            at = pl.ds(pl.multiple_of(base + t * tile, tile), tile)
            return jnp.dot(rows_x[...], weights[:, at], preferred_element_type=jnp.float32)

        def peers(t, carry):
            at = pl.multiple_of(t * tile, tile)
            gu_send[q, :, pl.ds(at, tile)] = product(gate_w, (1 - sec) * half, t).astype(jnp.bfloat16)
            gu_send[q, :, pl.ds(at + half, tile)] = product(up_w, (1 - sec) * half, t).astype(jnp.bfloat16)
            return carry

        def mine(t, carry):
            at = pl.multiple_of(t * tile, tile)
            gu_own[q, :, pl.ds(at, tile)] = product(gate_w, sec * half, t)
            gu_own[q, :, pl.ds(at + half, tile)] = product(up_w, sec * half, t)
            return carry

        lax.fori_loop(0, half // tile, peers, 0)
        send(gu_send.at[q], gu_recv.at[q], x_send.at[q], x_recv.at[q], {"sec": 1 - sec})
        lax.fori_loop(0, half // tile, mine, 0)

    def activate(q):
        wait_for(gu_recv.at[q], x_recv.at[q])
        full = gu_own[q] + gu_recv[q].astype(jnp.float32)
        gate, up = full[:, :half], full[:, half:]
        hidden[sec, q] = (gate / (1.0 + jnp.exp(-gate)) * up).astype(jnp.bfloat16)
        send(hidden.at[sec, q], hidden.at[sec, q], h_send.at[q], h_recv.at[q], {"sec": 1 - sec})

    def down(q):
        wait_for(hidden.at[1 - sec, q], h_recv.at[q])
        if q == 0:
            loads[2].wait()
        first = first_slot(q)
        both = jnp.concatenate([hidden[0, q], hidden[1, q]], axis=1)
        wide = [
            jnp.dot(both, down_w[:, c * width:(c + 1) * width], preferred_element_type=jnp.float32).astype(
                jnp.bfloat16
            )
            for c in range(SPLIT)
        ]
        for u in range(block * members // PAIR):
            tall = jnp.concatenate([w[u * PAIR * CAP:(u + 1) * PAIR * CAP] for w in wide], axis=0)
            flat = jnp.dot(order_t[...], tall, preferred_element_type=jnp.float32).astype(jnp.bfloat16)
            for s in range(PAIR):
                at = first + u * PAIR + s
                parts[at // members, at % members] = flat[s * UNIT:(s + 1) * UNIT]
        start = first // members
        for g in range(1, members):
            to = (j + g) % members
            send(
                parts.at[pl.ds(start, block), to], group_parts.at[g - 1, pl.ds(start, block)],
                g_send.at[q, g - 1], g_recv.at[q, g - 1], on_ctx(e * members + to),
            )

    def give_back(q):
        start = first_slot(q) // members
        for g in range(1, members):
            wait_for(group_parts.at[g - 1, pl.ds(start, block)], g_recv.at[q, g - 1])
        for i in range(block):
            source = expert_at(q, i, -1)
            total = parts[source, j].astype(jnp.float32)
            for g in range(1, members):
                total = total + group_parts[g - 1, source].astype(jnp.float32)
            if (q, i) == last:
                returned[e] = total.astype(jnp.bfloat16)
            else:
                back[source] = total.astype(jnp.bfloat16)
                send(
                    back.at[source], returned.at[e], r_send.at[q * block + i], r_recv.at[e],
                    on_ctx(source * members + j),
                )

    stages = (forward, gate_up, activate, down, give_back)
    lag = (0, 0, 1, 1, 2)
    for step in range(CHUNKS + max(lag)):
        for stage, delay in sorted(zip(stages, lag), key=lambda pair: pair[1]):
            if 0 <= step - delay < CHUNKS:
                stage(step - delay)

    for q, i in others:
        target = expert_at(q, i, 1)
        wait_for(returned.at[target], r_recv.at[target])
    flat = returned[...].reshape(EXPERTS * UNIT, width)
    for c in range(SPLIT):
        both = jnp.dot(
            mix[c * 2 * tokens:(c + 1) * 2 * tokens, :], flat, preferred_element_type=jnp.float32
        )
        out_ref[:, c * width:(c + 1) * width] = (both[:tokens] + both[tokens:]).astype(jnp.bfloat16)
    for copy in sent:
        copy.wait_send()


def run_experts(normed, logits, routes, w_gate, w_up, w_down, n):
    tokens, wide = normed.shape
    width = wide // SPLIT
    members = n // EXPERTS
    ff = w_gate.shape[1]
    chunk_rows = n * CAP // CHUNKS
    block = EXPERTS // CHUNKS
    vmem = pl.BlockSpec(memory_space=pltpu.VMEM)
    any_spec = pl.BlockSpec(memory_space=pltpu.HBM)
    bf16 = jnp.bfloat16
    dma = pltpu.SemaphoreType.DMA
    more = max(members - 1, 1)
    return pl.pallas_call(
        functools.partial(experts_kernel, n),
        out_shape=jax.ShapeDtypeStruct((tokens, wide), bf16),
        in_specs=[vmem] * 3 + [any_spec] * 3,
        out_specs=vmem,
        scratch_shapes=[
            pltpu.VMEM((PAIR * UNIT, PAIR * UNIT), bf16),
            pltpu.VMEM((PAIR * UNIT, PAIR * UNIT), bf16),
            pltpu.VMEM((SPLIT * 2 * tokens, EXPERTS * UNIT), bf16),
            pltpu.VMEM(w_gate.shape, bf16),
            pltpu.VMEM(w_up.shape, bf16),
            pltpu.VMEM(w_down.shape, bf16),
            pltpu.VMEM((EXPERTS, UNIT, width), bf16),
            pltpu.VMEM((n, UNIT, width), bf16),
            pltpu.VMEM((chunk_rows, wide), bf16),
            pltpu.VMEM((CHUNKS, chunk_rows, ff), bf16),
            pltpu.VMEM((CHUNKS, chunk_rows, ff), jnp.float32),
            pltpu.VMEM((CHUNKS, chunk_rows, ff), bf16),
            pltpu.VMEM((2, CHUNKS, chunk_rows, ff // 2), bf16),
            pltpu.VMEM((EXPERTS, members, UNIT, width), bf16),
            pltpu.VMEM((more, EXPERTS, UNIT, width), bf16),
            pltpu.VMEM((EXPERTS, UNIT, width), bf16),
            pltpu.VMEM((EXPERTS, UNIT, width), bf16),
            dma((3,)),
            dma((1,)),
            dma((EXPERTS,)),
            dma((EXPERTS, more)),
            dma((n,)),
            dma((CHUNKS,)),
            dma((CHUNKS,)),
            dma((CHUNKS,)),
            dma((CHUNKS,)),
            dma((CHUNKS, more)),
            dma((CHUNKS, more)),
            dma((EXPERTS,)),
            dma((EXPERTS,)),
        ],
        compiler_params=pltpu.CompilerParams(
            collective_id=1, has_side_effects=True, vmem_limit_bytes=63 << 20
        ),
        name="experts",
    )(normed, logits, routes.T, w_gate, w_up, w_down)


def on_device(queries, keys, values, gain, router, w_gate, w_up, w_down, routes):
    cycle_size = lax.axis_size("ctx")
    token_count = queries.shape[0]
    normed, logits = attend(queries, keys, values, gain, router, cycle_size)
    if cycle_size * CAP <= 640:
        return (normed, run_experts(normed, logits, routes, w_gate, w_up, w_down, cycle_size))
    logits = logits[:, :EXPERTS]
    expert_ids = jnp.arange(EXPERTS, dtype=jnp.int32)
    picks = (routes[:, :, None] == expert_ids[None, None, :]).astype(jnp.float32)
    chosen = jnp.sum(picks * logits[:, None, :], axis=2)
    combine = 1.0 / jnp.sum(jnp.exp(chosen[:, None, :] - chosen[:, :, None]), axis=2)
    flat_routes = routes.reshape(token_count * TOP)
    hot = (flat_routes[:, None] == expert_ids[None, :]).astype(jnp.int32)
    before = jnp.cumsum(hot, axis=0) - hot
    slots = jnp.sum(before * hot, axis=1)
    cells = flat_routes * CAP + slots
    placing = (cells[:, None] == jnp.arange(EXPERTS * CAP, dtype=jnp.int32)[None, :]).astype(
        jnp.float32
    )
    placing = placing.reshape(token_count, TOP, EXPERTS * CAP)
    token_place = jnp.sum(placing, axis=1).astype(jnp.bfloat16)
    width_local = normed.shape[1]
    packed = jnp.einsum(
        "tc,td->cd", token_place, normed, preferred_element_type=jnp.float32
    ).astype(jnp.bfloat16)
    group_count = cycle_size // EXPERTS
    outgoing = jnp.broadcast_to(
        packed.reshape(EXPERTS, 1, CAP, width_local), (EXPERTS, group_count, CAP, width_local)
    )
    outgoing = outgoing.reshape(cycle_size, CAP, width_local)
    received = lax.all_to_all(outgoing, "ctx", split_axis=0, concat_axis=0, tiled=True)
    gate_part = jnp.einsum("sid,df->sif", received, w_gate, preferred_element_type=jnp.float32)
    up_part = jnp.einsum("sid,df->sif", received, w_up, preferred_element_type=jnp.float32)
    gate_full = lax.psum(gate_part.astype(jnp.bfloat16), "sec").astype(jnp.float32)
    up_full = lax.psum(up_part.astype(jnp.bfloat16), "sec").astype(jnp.float32)
    hidden = (jax.nn.silu(gate_full) * up_full).astype(jnp.bfloat16)
    down_part = jnp.einsum(
        "sif,fd->sid", hidden, w_down, preferred_element_type=jnp.float32
    ).astype(jnp.bfloat16)
    returned = lax.all_to_all(down_part, "ctx", split_axis=0, concat_axis=0, tiled=True)
    summed = jnp.sum(
        returned.reshape(EXPERTS, group_count, CAP, width_local).astype(jnp.float32), axis=1
    )
    summed = summed.reshape(EXPERTS * CAP, width_local)
    mixing = jnp.sum(placing * combine[:, :, None], axis=1)
    moe_out = jnp.dot(mixing, summed, precision=lax.Precision.HIGHEST).astype(jnp.bfloat16)
    return (normed, moe_out)


def solution(mesh):
    in_specs = (
        P("ctx", "sec"),
        P("ctx", "sec"),
        P("ctx", "sec"),
        P("sec"),
        P("sec", None),
        P("sec", "ctx"),
        P("sec", "ctx"),
        P("ctx", "sec"),
        P("ctx", None),
    )
    out_specs = (P("ctx", "sec"), P("ctx", "sec"))
    return jax.shard_map(
        on_device, mesh=mesh, in_specs=in_specs, out_specs=out_specs, check_vma=False
    )
```
